32 devices in a mesh: groups: 1, blk: 16 (over z, y, core), pts: 2 (over x).
Axes of the slice: x: 2, y: 2, z: 4, core: 2. Of those that a mesh axis runs over, the one named last changes fastest.
Arguments:
- gen_points: float32 [16, 3, 1024], P(('groups', 'blk'), None, 'pts'), may hold values from -5 to 5, as said below
- ref_points: float32 [128, 3, 1024], P(('groups', 'blk'), None, 'pts'), may hold values from -5 to 5, as said below
Outputs:
- chamfer: float32 [16, 128], P(('groups', 'blk'))
The draws below stay inside these ranges and needn't reach their ends.
Inputs may be any that keep to these rules, and one draw needn't show every extreme that they name: `gen_points`: each shape is a cloud of points around a centre of its own, with a spread of its own. `ref_points`: each shape is a cloud of points around a centre of its own, with a spread of its own.
All inputs are finite; a program needn't handle non-finite values.
Results may differ from the reference program's by a relative error of at most 0.00002.
Values sent between devices are 32-bit elements; how exact they have to be, the bound alone decides.
A program may use at most 64 MiB of HBM per device.

```python
import math
import jax
import jax.numpy as jnp
from jax import lax

P_SIZE = 1024
G = 16
R = 128


def shape_cloud(key, count):
    key_centre, key_spread, key_noise = jax.random.split(key, 3)
    centres = jax.random.uniform(key_centre, (count, 3, 1), jnp.float32, -1.0, 1.0)
    spread = jnp.exp(jax.random.uniform(key_spread, (count, 1, 1), jnp.float32, math.log(0.3), 0.0))
    noise = jnp.clip(jax.random.normal(key_noise, (count, 3, P_SIZE), jnp.float32), -4.0, 4.0)
    return centres + spread * noise


def draw_gen_points(key, part):
    return shape_cloud(jax.random.fold_in(key, 11), G)


def draw_ref_points(key, part):
    return shape_cloud(jax.random.fold_in(key, 23), R)


def setup_inputs(seed: int = 0, part: int = 0) -> dict:
    key_list = jax.random.split(jax.random.key(seed), 3)
    part_splits = jax.random.split(jax.random.fold_in(key_list[2], part), 3)
    gen_points = draw_gen_points(jax.random.fold_in(jax.random.fold_in(key_list[2], part), 71), part)
    ref_points = draw_ref_points(jax.random.fold_in(jax.random.fold_in(key_list[2], part), 71), part)
    return {"gen_points": gen_points, "ref_points": ref_points}


def pair_terms(gen_points, one_ref):
    diff_x = gen_points[:, 0, :, None] - one_ref[0][None, None, :]
    diff_y = gen_points[:, 1, :, None] - one_ref[1][None, None, :]
    diff_z = gen_points[:, 2, :, None] - one_ref[2][None, None, :]
    dist = diff_x * diff_x + diff_y * diff_y + diff_z * diff_z
    forward = jnp.mean(jnp.min(dist, axis=2), axis=1)
    backward = jnp.mean(jnp.min(dist, axis=1), axis=1)
    return forward + backward


def reference(gen_points, ref_points):
    columns = lax.map(lambda one_ref: pair_terms(gen_points, one_ref), ref_points)
    return jnp.transpose(columns)
```

```python
import functools

import jax
import jax.numpy as jnp
from jax import lax
from jax.experimental import pallas as pl
from jax.experimental.pallas import tpu as pltpu
from jax.sharding import PartitionSpec as P

MESH = pl.DeviceIdType.MESH

DEPTH = 48


def split3(value):
    high = value.astype(jnp.bfloat16).astype(jnp.float32)
    middle = (value - high).astype(jnp.bfloat16).astype(jnp.float32)
    return high, middle, value - high - middle


def gen_rows(points, norm):
    n = points.shape[1]
    one, zero = jnp.ones((1, n), jnp.float32), jnp.zeros((1, n), jnp.float32)
    ph, pm, pl_ = split3(points)
    nh, nm, nl = split3(norm)
    tile = lambda p, c, q: jnp.concatenate([p, c, q, jnp.zeros((3, n), jnp.float32)], axis=0)
    stack = [
        tile(ph, one, nh), tile(pm, zero, nm), tile(pl_, zero, nl),
        tile(ph, one, zero), tile(pm, zero, zero), tile(ph, one, zero),
        jnp.zeros((128 - DEPTH, n), jnp.float32),
    ]
    return jnp.concatenate(stack, axis=0).T.astype(jnp.bfloat16)


def ref_rows(doubled, norm):
    n = doubled.shape[1]
    rows = jnp.concatenate([doubled, norm, jnp.ones((1, n), jnp.float32), jnp.zeros((3, n), jnp.float32)], axis=0)
    h, m, l = split3(rows)
    return jnp.concatenate([h, h, h, m, m, l], axis=0).astype(jnp.bfloat16)


def spread_gen(points, norm):
    count = points.shape[1]
    stack = jnp.concatenate([points, norm, jnp.zeros((124, count), jnp.float32)], axis=0).T
    return [jnp.broadcast_to(stack[:, c : c + 1], (count, 128)) for c in range(4)]


def pair_sums(rows_ref, gen, cols, wide_gen, wide_ref, n, mc, nc, vec):
    fsum = jnp.zeros((8, 128), jnp.float32)
    blocks = n // 128
    back = [None] * blocks
    chunks = (n - vec) // mc
    vec_tiles = vec // 8
    wide_back = [None] * blocks
    done = 0
    for ic in range(chunks):
        a = rows_ref[pl.ds(gen * n + ic * mc, mc), 0:DEPTH]
        acc = None
        for jc in range(n // nc):
            d = jnp.dot(a, cols[:, jc * nc : (jc + 1) * nc], preferred_element_type=jnp.float32)
            for q in range(nc // 128):
                part = d[:, q * 128 : (q + 1) * 128]
                acc = part if acc is None else jnp.minimum(acc, part)
                k = jc * (nc // 128) + q
                down = jnp.min(part.reshape(mc // 8, 8, 128), axis=0)
                back[k] = down if back[k] is None else jnp.minimum(back[k], down)
        near = jnp.broadcast_to(jnp.min(acc, axis=1, keepdims=True), (mc, 128))
        fsum = fsum + jnp.sum(near.reshape(mc // 8, 8, 128), axis=0)
        upto = vec_tiles * (ic + 1) // chunks
        for tile in range(done, upto):
            ax, ay, az, an = (wide_gen[gen, c, pl.ds(tile * 8, 8), :] for c in range(4))
            acc = None
            for k in range(blocks):
                bx, by, bz, bn = (wide_ref[c, :, pl.ds(k * 128, 128)] for c in range(4))
                cross = ax * bx + ay * by + az * bz
                u = cross + bn
                w = cross + an
                acc = u if acc is None else jnp.minimum(acc, u)
                wide_back[k] = w if wide_back[k] is None else jnp.minimum(wide_back[k], w)
            fsum = fsum + jnp.broadcast_to(jnp.min(acc, axis=1, keepdims=True), (8, 128)) + an
        done = upto
    far = None
    for k in range(blocks):
        down = back[k]
        if vec:
            down = jnp.minimum(down, wide_back[k] + wide_ref[3, :, pl.ds(k * 128, 128)])
        low = jnp.min(down, axis=0, keepdims=True)
        far = low if far is None else far + low
    return jnp.sum(fsum, axis=0, keepdims=True) + jnp.sum(far, axis=1, keepdims=True)


def kernel(sizes, gen_ref, ref_ref, out_ref, gbuf, rbuf, rows, wide_gen, wide_ref, res, obuf, g_send, g_recv, r_send, r_recv, o_send, o_recv):
    outer, inner, halves, chunk, n, mc, nc, vec = sizes
    blk, x = lax.axis_index("blk"), lax.axis_index("pts")
    bo, bi = blk // inner, blk % inner
    width = res.shape[2]
    plane = [(i, h) for i in range(inner) for h in range(halves) if (i, h) != (0, 0)]
    column = [(o, h) for o in range(outer) for h in range(halves) if (o, h) != (0, 0)]

    def plane_id(i, h):
        return lax.rem(bi + i, inner), lax.rem(x + h, halves)

    def column_id(o, h):
        return lax.rem(bo + o, outer), lax.rem(x + h, halves)

    barrier = pltpu.get_barrier_semaphore()
    for i, h in plane:
        ti, th = plane_id(i, h)
        pl.semaphore_signal(barrier, device_id={"blk": bo * inner + ti, "pts": th}, device_id_type=MESH)
    for o, h in column:
        if o:
            to, th = column_id(o, h)
            pl.semaphore_signal(barrier, device_id={"blk": to * inner + bi, "pts": th}, device_id_type=MESH)
    pl.semaphore_wait(barrier, len(plane) + len(column) - (halves - 1))

    copies = []
    for s, (i, h) in enumerate(plane):
        ti, th = plane_id(i, h)
        copies.append(
            pltpu.make_async_remote_copy(
                src_ref=gen_ref.at[0], dst_ref=gbuf.at[bi, x], send_sem=g_send.at[s], recv_sem=g_recv.at[bi, x],
                device_id={"blk": bo * inner + ti, "pts": th}, device_id_type=MESH,
            )
        )
    for s, (o, h) in enumerate(column):
        to, th = column_id(o, h)
        copies.append(
            pltpu.make_async_remote_copy(
                src_ref=ref_ref.at[pl.ds(th * chunk, chunk)], dst_ref=rbuf.at[bo, x], send_sem=r_send.at[s],
                recv_sem=r_recv.at[bo, x], device_id={"blk": to * inner + bi, "pts": th}, device_id_type=MESH,
            )
        )
    for copy in copies:
        copy.start()
    own_gen = pltpu.make_async_copy(gen_ref.at[0], gbuf.at[bi, x], g_recv.at[bi, x])
    own_ref = pltpu.make_async_copy(ref_ref.at[pl.ds(x * chunk, chunk)], rbuf.at[bo, x], r_recv.at[bo, x])
    own_gen.start()
    own_ref.start()

    for i in range(inner):
        for h in range(halves):
            pltpu.make_async_copy(gen_ref.at[0], gbuf.at[i, h], g_recv.at[i, h]).wait()
    for i in range(inner):
        points = jnp.concatenate([gbuf[i, h] for h in range(halves)], axis=1)
        norm = jnp.sum(points * points, axis=0, keepdims=True)
        rows[pl.ds(i * n, n), :] = gen_rows(points, norm)
        if vec:
            for c, wide in enumerate(spread_gen(points[:, n - vec :], norm[:, n - vec :])):
                wide_gen[i, c] = wide
    res[...] = jnp.zeros_like(res)
    lane = lax.broadcasted_iota(jnp.int32, (8, width), 1)

    def some_refs(step, carry):
        o = lax.rem(bo + step, outer)
        for h in range(halves):
            pltpu.make_async_copy(ref_ref.at[pl.ds(0, chunk)], rbuf.at[o, h], r_recv.at[o, h]).wait()

        def one_ref(c, carry):
            points = jnp.concatenate([rbuf[o, h, c] for h in range(halves)], axis=1)
            norm = jnp.sum(points * points, axis=0, keepdims=True)
            points = -2.0 * points
            cols = ref_rows(points, norm)
            if vec:
                for k in range(3):
                    wide_ref[k] = jnp.broadcast_to(points[k : k + 1], (8, n))
                wide_ref[3] = jnp.broadcast_to(norm, (8, n))
            place = lane == (o * inner + bi) * chunk * halves + x * chunk + c
            for i in range(inner):
                value = pair_sums(rows, i, cols, wide_gen, wide_ref, n, mc, nc, vec) * (1.0 / n)
                value = jnp.concatenate([value] * (width // 128), axis=1)
                res[i] = jnp.where(place, jnp.broadcast_to(value, (8, width)), res[i])
            return carry

        return lax.fori_loop(0, chunk, one_ref, carry)

    lax.fori_loop(0, outer, some_refs, 0)

    answers = []
    for s, (i, h) in enumerate(plane):
        ti, th = plane_id(i, h)
        answers.append(
            pltpu.make_async_remote_copy(
                src_ref=res.at[ti], dst_ref=obuf.at[bi, x], send_sem=o_send.at[s], recv_sem=o_recv.at[bi, x],
                device_id={"blk": bo * inner + ti, "pts": th}, device_id_type=MESH,
            )
        )
    for copy in answers:
        copy.start()
    total = res[bi]
    for i, h in plane:
        ti, th = plane_id(i, h)
        pltpu.make_async_copy(res.at[0], obuf.at[ti, th], o_recv.at[ti, th]).wait()
        total = total + obuf[ti, th]
    out_ref[...] = total[0:1]
    for copy in copies:
        copy.wait_send()
    for copy in answers:
        copy.wait_send()


def split_of(blk_count, pts_count, refs):
    for inner in (4, 2, 1):
        if blk_count % inner == 0:
            return blk_count // inner, inner


def shards(gen_points, ref_points):
    halves, blk_count = lax.axis_size("pts"), lax.axis_size("blk")
    refs, _, share = ref_points.shape
    n = share * halves
    outer, inner = split_of(blk_count, halves, refs)
    chunk = refs // halves
    width = refs * blk_count
    vec = 0
    sizes = (outer, inner, halves, chunk, n, 256, 256, vec)
    return pl.pallas_call(
        functools.partial(kernel, sizes),
        out_shape=jax.ShapeDtypeStruct((1, width), jnp.float32),
        in_specs=[pl.BlockSpec(memory_space=pltpu.VMEM)] * 2,
        out_specs=pl.BlockSpec(memory_space=pltpu.VMEM),
        scratch_shapes=[
            pltpu.VMEM((inner, halves, 3, share), jnp.float32),
            pltpu.VMEM((outer, halves, chunk, 3, share), jnp.float32),
            pltpu.VMEM((inner * n, 128), jnp.bfloat16),
            pltpu.VMEM((inner, 4, max(vec, 8), 128), jnp.float32),
            pltpu.VMEM((4, 8, n), jnp.float32),
            pltpu.VMEM((inner, 8, width), jnp.float32),
            pltpu.VMEM((inner, halves, 8, width), jnp.float32),
            pltpu.SemaphoreType.DMA((inner * halves,)),
            pltpu.SemaphoreType.DMA((inner, halves)),
            pltpu.SemaphoreType.DMA((outer * halves,)),
            pltpu.SemaphoreType.DMA((outer, halves)),
            pltpu.SemaphoreType.DMA((inner * halves,)),
            pltpu.SemaphoreType.DMA((inner, halves)),
        ],
        compiler_params=pltpu.CompilerParams(collective_id=0, has_side_effects=True),
        name="chamfer",
    )(gen_points, ref_points)


def solution(mesh):
    placed = (P(("groups", "blk"), None, "pts"), P(("groups", "blk"), None, "pts"))
    return jax.shard_map(
        shards, mesh=mesh, in_specs=placed, out_specs=P(("groups", "blk"), None), check_vma=False
    )
```

```python
import functools

import jax
import jax.numpy as jnp
from jax import lax
from jax.experimental import pallas as pl
from jax.experimental.pallas import tpu as pltpu
from jax.sharding import PartitionSpec as P

MESH = pl.DeviceIdType.MESH

DEPTH = 48


def split3(value):
    high = value.astype(jnp.bfloat16).astype(jnp.float32)
    middle = (value - high).astype(jnp.bfloat16).astype(jnp.float32)
    return high, middle, value - high - middle


def gen_rows(points, norm):
    n = points.shape[1]
    one, zero = jnp.ones((1, n), jnp.float32), jnp.zeros((1, n), jnp.float32)
    ph, pm, pl_ = split3(points)
    nh, nm, nl = split3(norm)
    tile = lambda p, c, q: jnp.concatenate([p, c, q, jnp.zeros((3, n), jnp.float32)], axis=0)
    stack = [
        tile(ph, one, nh), tile(pm, zero, nm), tile(pl_, zero, nl),
        tile(ph, one, zero), tile(pm, zero, zero), tile(ph, one, zero),
        jnp.zeros((128 - DEPTH, n), jnp.float32),
    ]
    return jnp.concatenate(stack, axis=0).T.astype(jnp.bfloat16)


def ref_rows(doubled, norm):
    n = doubled.shape[1]
    rows = jnp.concatenate([doubled, norm, jnp.ones((1, n), jnp.float32), jnp.zeros((3, n), jnp.float32)], axis=0)
    h, m, l = split3(rows)
    return jnp.concatenate([h, h, h, m, m, l], axis=0).astype(jnp.bfloat16)


def spread_gen(points, norm):
    count = points.shape[1]
    stack = jnp.concatenate([points, norm, jnp.zeros((124, count), jnp.float32)], axis=0).T
    return [jnp.broadcast_to(stack[:, c : c + 1], (count, 128)) for c in range(4)]


def pair_sums(rows_ref, gen, cols, wide_gen, wide_ref, n, mc, nc, vec):
    fsum = jnp.zeros((8, 128), jnp.float32)
    blocks = n // 128
    back = [None] * blocks
    chunks = (n - vec) // mc
    vec_tiles = vec // 8
    wide_back = [None] * blocks
    done = 0
    for ic in range(chunks):
        a = rows_ref[pl.ds(gen * n + ic * mc, mc), 0:DEPTH]
        acc = None
        for jc in range(n // nc):
            d = jnp.dot(a, cols[:, jc * nc : (jc + 1) * nc], preferred_element_type=jnp.float32)
            for q in range(nc // 128):
                part = d[:, q * 128 : (q + 1) * 128]
                acc = part if acc is None else jnp.minimum(acc, part)
                k = jc * (nc // 128) + q
                down = jnp.min(part.reshape(mc // 8, 8, 128), axis=0)
                back[k] = down if back[k] is None else jnp.minimum(back[k], down)
        near = jnp.broadcast_to(jnp.min(acc, axis=1, keepdims=True), (mc, 128))
        fsum = fsum + jnp.sum(near.reshape(mc // 8, 8, 128), axis=0)
        upto = vec_tiles * (ic + 1) // chunks
        for tile in range(done, upto):
            ax, ay, az, an = (wide_gen[gen, c, pl.ds(tile * 8, 8), :] for c in range(4))
            acc = None
            for k in range(blocks):
                bx, by, bz, bn = (wide_ref[c, :, pl.ds(k * 128, 128)] for c in range(4))
                cross = ax * bx + ay * by + az * bz
                u = cross + bn
                w = cross + an
                acc = u if acc is None else jnp.minimum(acc, u)
                wide_back[k] = w if wide_back[k] is None else jnp.minimum(wide_back[k], w)
            fsum = fsum + jnp.broadcast_to(jnp.min(acc, axis=1, keepdims=True), (8, 128)) + an
        done = upto
    far = None
    for k in range(blocks):
        down = back[k]
        if vec:
            down = jnp.minimum(down, wide_back[k] + wide_ref[3, :, pl.ds(k * 128, 128)])
        low = jnp.min(down, axis=0, keepdims=True)
        far = low if far is None else far + low
    return jnp.sum(fsum, axis=0, keepdims=True) + jnp.sum(far, axis=1, keepdims=True)


def kernel(sizes, gen_in, ref_in, out_ref, gen_ref, ref_ref, gbuf, rbuf, rows, wide_gen, wide_ref, res, obuf, g_send, g_recv, r_send, r_recv, o_send, o_recv):
    outer, inner, halves, chunk, n, mc, nc, vec = sizes
    blk, x = lax.axis_index("blk"), lax.axis_index("pts")
    bo, bi = blk // inner, blk % inner
    width = res.shape[2]
    plane = [(i, h) for i in range(inner) for h in range(halves) if (i, h) != (0, 0)]
    column = [(o, h) for o in range(outer) for h in range(halves) if (o, h) != (0, 0)]

    def plane_id(i, h):
        return lax.rem(bi + i, inner), lax.rem(x + h, halves)

    def column_id(o, h):
        return lax.rem(bo + o, outer), lax.rem(x + h, halves)

    for k in range(3):
        gen_ref[0, k : k + 1, :] = gen_in[k]
        for c in range(halves * chunk):
            ref_ref[c // chunk, c % chunk, k : k + 1, :] = ref_in[k, c : c + 1, :]

    barrier = pltpu.get_barrier_semaphore()
    for i, h in plane:
        ti, th = plane_id(i, h)
        pl.semaphore_signal(barrier, device_id={"blk": bo * inner + ti, "pts": th}, device_id_type=MESH)
    for o, h in column:
        if o:
            to, th = column_id(o, h)
            pl.semaphore_signal(barrier, device_id={"blk": to * inner + bi, "pts": th}, device_id_type=MESH)
    pl.semaphore_wait(barrier, len(plane) + len(column) - (halves - 1))

    copies = []
    for s, (i, h) in enumerate(plane):
        ti, th = plane_id(i, h)
        copies.append(
            pltpu.make_async_remote_copy(
                src_ref=gen_ref.at[0], dst_ref=gbuf.at[bi, x], send_sem=g_send.at[s], recv_sem=g_recv.at[bi, x],
                device_id={"blk": bo * inner + ti, "pts": th}, device_id_type=MESH,
            )
        )
    for s, (o, h) in enumerate(column):
        to, th = column_id(o, h)
        copies.append(
            pltpu.make_async_remote_copy(
                src_ref=ref_ref.at[th], dst_ref=rbuf.at[bo, x], send_sem=r_send.at[s],
                recv_sem=r_recv.at[bo, x], device_id={"blk": to * inner + bi, "pts": th}, device_id_type=MESH,
            )
        )
    for copy in copies:
        copy.start()
    own_gen = pltpu.make_async_copy(gen_ref.at[0], gbuf.at[bi, x], g_recv.at[bi, x])
    own_ref = pltpu.make_async_copy(ref_ref.at[x], rbuf.at[bo, x], r_recv.at[bo, x])
    own_gen.start()
    own_ref.start()

    for step in range(inner):
        i = lax.rem(bi + step, inner)
        for h in range(halves):
            pltpu.make_async_copy(gen_ref.at[0], gbuf.at[i, h], g_recv.at[i, h]).wait()
        points = jnp.concatenate([gbuf[i, h] for h in range(halves)], axis=1)
        norm = jnp.sum(points * points, axis=0, keepdims=True)
        rows[pl.ds(pl.multiple_of(i * n, n), n), :] = gen_rows(points, norm)
        if vec:
            for c, wide in enumerate(spread_gen(points[:, n - vec :], norm[:, n - vec :])):
                wide_gen[i, c] = wide
    res[...] = jnp.zeros_like(res)
    lane = lax.broadcasted_iota(jnp.int32, (8, width), 1)

    def some_refs(step, carry):
        o = lax.rem(bo + step, outer)
        for h in range(halves):
            pltpu.make_async_copy(ref_ref.at[0], rbuf.at[o, h], r_recv.at[o, h]).wait()

        def one_ref(c, carry):
            points = jnp.concatenate([rbuf[o, h, c] for h in range(halves)], axis=1)
            norm = jnp.sum(points * points, axis=0, keepdims=True)
            points = -2.0 * points
            cols = ref_rows(points, norm)
            if vec:
                for k in range(3):
                    wide_ref[k] = jnp.broadcast_to(points[k : k + 1], (8, n))
                wide_ref[3] = jnp.broadcast_to(norm, (8, n))
            place = lane == (o * inner + bi) * chunk * halves + x * chunk + c
            for i in range(inner):
                value = pair_sums(rows, i, cols, wide_gen, wide_ref, n, mc, nc, vec) * (1.0 / n)
                value = jnp.concatenate([value] * (width // 128), axis=1)
                res[i] = jnp.where(place, jnp.broadcast_to(value, (8, width)), res[i])
            return carry

        return lax.fori_loop(0, chunk, one_ref, carry)

    lax.fori_loop(0, outer, some_refs, 0)

    answers = []
    for s, (i, h) in enumerate(plane):
        ti, th = plane_id(i, h)
        answers.append(
            pltpu.make_async_remote_copy(
                src_ref=res.at[ti], dst_ref=obuf.at[bi, x], send_sem=o_send.at[s], recv_sem=o_recv.at[bi, x],
                device_id={"blk": bo * inner + ti, "pts": th}, device_id_type=MESH,
            )
        )
    for copy in answers:
        copy.start()
    total = res[bi]
    for i, h in plane:
        ti, th = plane_id(i, h)
        pltpu.make_async_copy(res.at[0], obuf.at[ti, th], o_recv.at[ti, th]).wait()
        total = total + obuf[ti, th]
    out_ref[...] = total[0:1]
    for copy in copies:
        copy.wait_send()
    for copy in answers:
        copy.wait_send()


def split_of(blk_count, pts_count, refs):
    for inner in (4, 2, 1):
        if blk_count % inner == 0:
            return blk_count // inner, inner


def shards(gen_points, ref_points):
    halves, blk_count = lax.axis_size("pts"), lax.axis_size("blk")
    refs, _, share = ref_points.shape
    n = share * halves
    outer, inner = split_of(blk_count, halves, refs)
    chunk = refs // halves
    width = refs * blk_count
    vec = 0
    sizes = (outer, inner, halves, chunk, n, 256, 256, vec)
    return pl.pallas_call(
        functools.partial(kernel, sizes),
        out_shape=jax.ShapeDtypeStruct((1, width), jnp.float32),
        in_specs=[pl.BlockSpec(memory_space=pltpu.VMEM)] * 2,
        out_specs=pl.BlockSpec(memory_space=pltpu.VMEM),
        scratch_shapes=[
            pltpu.VMEM((1, 3, share), jnp.float32),
            pltpu.VMEM((halves, chunk, 3, share), jnp.float32),
            pltpu.VMEM((inner, halves, 3, share), jnp.float32),
            pltpu.VMEM((outer, halves, chunk, 3, share), jnp.float32),
            pltpu.VMEM((inner * n, 128), jnp.bfloat16),
            pltpu.VMEM((inner, 4, max(vec, 8), 128), jnp.float32),
            pltpu.VMEM((4, 8, n), jnp.float32),
            pltpu.VMEM((inner, 8, width), jnp.float32),
            pltpu.VMEM((inner, halves, 8, width), jnp.float32),
            pltpu.SemaphoreType.DMA((inner * halves,)),
            pltpu.SemaphoreType.DMA((inner, halves)),
            pltpu.SemaphoreType.DMA((outer * halves,)),
            pltpu.SemaphoreType.DMA((outer, halves)),
            pltpu.SemaphoreType.DMA((inner * halves,)),
            pltpu.SemaphoreType.DMA((inner, halves)),
        ],
        compiler_params=pltpu.CompilerParams(collective_id=0, has_side_effects=True),
        name="chamfer",
    )(jnp.transpose(gen_points, (1, 0, 2)), jnp.transpose(ref_points, (1, 0, 2)))


def solution(mesh):
    placed = (P(("groups", "blk"), None, "pts"), P(("groups", "blk"), None, "pts"))
    return jax.shard_map(
        shards, mesh=mesh, in_specs=placed, out_specs=P(("groups", "blk"), None), check_vma=False
    )
```
